256 devices in a mesh: seq: 32 (over x, y, z_lo), dp: 8 (over z_hi, core).
Axes of the slice: x: 4, y: 4, z: 8 (z_hi: 4, z_lo: 2; z = z_hi * 2 + z_lo), core: 2. Of those that a mesh axis runs over, the one named last changes fastest.
Arguments:
- queries: bfloat16 [16, 2048, 4096], P('dp', 'seq'), may hold values from -300 to 300
- key_states: bfloat16 [16, 2048, 4096], P('dp', 'seq'), may hold values from -4.5 to 4.5
- value_states: bfloat16 [16, 2048, 4096], P('dp', 'seq'), may hold values from -6 to 6
- grad_output: bfloat16 [16, 2048, 4096], P('dp', 'seq'), may hold values from -6 to 6
- query_bias: bfloat16 [4096], P(('seq', 'dp')), may hold values from -5 to 5
Outputs:
- grad_queries: bfloat16 [16, 2048, 4096], P('dp', 'seq')
- grad_keys: bfloat16 [16, 2048, 4096], P('dp', 'seq')
- grad_values: bfloat16 [16, 2048, 4096], P('dp', 'seq')
- grad_bias: float32 [4096], P(('seq', 'dp'))
The draws below stay inside these ranges and needn't reach their ends.
All inputs are finite; a program needn't handle non-finite values.
Results may differ from the reference program's by a relative error of at most 0.007.
Values may be sent and summed in bfloat16 or wider, within the bound.
No kernel may reach another device: no remote copies, remote signals or barrier semaphores. Data moves between devices by JAX's collectives and lax.ppermute only.
A program may use at most 128 MiB of HBM per device.

```python
import math
import jax
import jax.numpy as jnp
from jax import lax

HDIM = 128
QBLOCKS = 4
WIDTH = 4096
SEQ_LEN = 2048
SEQS = 16


def key_values(key):
    base_values = jax.random.normal(jax.random.fold_in(key, 11), (SEQS, SEQ_LEN, WIDTH), jnp.float32)
    base_values = jnp.clip(base_values, -4.5, 4.5)
    return base_values


def draw_key_states(key, part):
    return key_values(key).astype(jnp.bfloat16)


def draw_queries(key, part):
    base_values = jax.random.normal(jax.random.fold_in(key, 21), (SEQS, SEQ_LEN, WIDTH), jnp.float32)
    base_values = jnp.clip(base_values, -4.5, 4.5)
    return base_values.astype(jnp.bfloat16)


def block_levels(rng, shape, pieces, smallest, top_value):
    level, own = 1.0, jax.random.fold_in(rng, 6)
    for axis_at, shards_of in pieces:
        steps = jnp.exp(jax.random.uniform(jax.random.fold_in(own, axis_at), (shards_of,), jnp.float32, smallest / len(pieces), top_value / len(pieces)))
        level = level * jnp.repeat(steps, shape[axis_at] // shards_of).reshape([-1 if axis == axis_at else 1 for axis in range(len(shape))])
    return level


def noise(rng, shape, width, bound, cuts=(), kind=jnp.bfloat16):
    values = jax.random.normal(rng, shape, jnp.float32) * width
    if len(cuts) > 0:
        values = block_levels(rng, shape, cuts, -0.22, 0.18) * values
    return jnp.clip(values, min=-bound, max=bound).astype(kind)


def setup_inputs(seed: int = 0) -> dict:
    keys = jax.random.split(jax.random.key(seed), 6)
    queries = draw_queries(jax.random.fold_in(keys[5], 71), 0)
    key_states = draw_key_states(jax.random.fold_in(keys[5], 71), 0)
    value_states = noise(keys[2], (SEQS, SEQ_LEN, WIDTH), 1.0, 6.0, ((0, 8), (1, 32)))
    grad_output = noise(keys[3], (SEQS, SEQ_LEN, WIDTH), 1.0, 6.0, ((0, 8), (1, 32)))
    query_bias = noise(keys[4], (WIDTH,), 1.0, 5.0, ((0, 256),))
    return {"queries": queries, "key_states": key_states, "value_states": value_states, "grad_output": grad_output, "query_bias": query_bias}


masked_value = -1e+30

def attend(query_full, key_rows, value_rows, grad_rows):
    item_count, seq_length, total_cols = query_full.shape
    head_count = total_cols // HDIM

    def heads_view(values):
        return values.astype(jnp.float32).reshape(item_count, seq_length, head_count, HDIM)
    query_heads = heads_view(query_full)
    key_heads = heads_view(key_rows)
    value_heads = heads_view(value_rows)
    grad_heads = heads_view(grad_rows)
    factor = 1.0 / math.sqrt(HDIM)
    block_rows = seq_length // QBLOCKS
    high = lax.Precision.HIGHEST
    grad_keys = jnp.zeros((item_count, seq_length, head_count, HDIM), jnp.float32)
    grad_values = jnp.zeros((item_count, seq_length, head_count, HDIM), jnp.float32)
    query_parts = []
    for block_idx in range(QBLOCKS):
        row_start = block_idx * block_rows
        key_end = row_start + block_rows
        block_query = query_heads[:, row_start:key_end]
        seen_keys = key_heads[:, :key_end]
        seen_values = value_heads[:, :key_end]
        block_grad = grad_heads[:, row_start:key_end]
        scores = jnp.einsum('nqhd,nkhd->nhqk', block_query, seen_keys, precision=high) * factor
        row_ids = row_start + jnp.arange(block_rows)[:, None]
        key_ids = jnp.arange(key_end)[None, :]
        scores = jnp.where(key_ids <= row_ids, scores, masked_value)
        highest = lax.optimization_barrier(jnp.max(scores, axis=-1, keepdims=True))
        shifted = jnp.exp(scores - highest)
        weights = shifted / lax.optimization_barrier(jnp.sum(shifted, axis=-1, keepdims=True))
        grad_probs = jnp.einsum('nqhd,nkhd->nhqk', block_grad, seen_values, precision=high)
        row_dot = lax.optimization_barrier(jnp.sum(weights * grad_probs, axis=-1, keepdims=True))
        grad_scores = (weights * (grad_probs - row_dot) * factor).astype(jnp.bfloat16).astype(jnp.float32)
        weights_low = weights.astype(jnp.bfloat16).astype(jnp.float32)
        grad_values = grad_values.at[:, :key_end].add(jnp.einsum('nhqk,nqhd->nkhd', weights_low, block_grad, precision=high))
        grad_keys = grad_keys.at[:, :key_end].add(jnp.einsum('nhqk,nqhd->nkhd', grad_scores, block_query, precision=high))
        query_parts.append(jnp.einsum('nhqk,nkhd->nqhd', grad_scores, seen_keys, precision=high))
    grad_queries = jnp.concatenate(query_parts, axis=1)
    shape_out = (item_count, seq_length, total_cols)
    return (grad_queries.reshape(shape_out), grad_keys.reshape(shape_out), grad_values.reshape(shape_out))

def reference(queries, key_states, value_states, grad_output, query_bias):
    query_full = (queries.astype(jnp.float32) + query_bias.astype(jnp.float32)[None, None, :]).astype(jnp.bfloat16)

    def one_sequence(items):
        query_one, key_one, value_one, grad_one = items
        grad_q, grad_k, grad_v = attend(query_one[None], key_one[None], value_one[None], grad_one[None])
        return (grad_q[0].astype(jnp.bfloat16), grad_k[0].astype(jnp.bfloat16), grad_v[0].astype(jnp.bfloat16), lax.optimization_barrier(jnp.sum(grad_q[0], axis=0)))
    grad_queries, grad_keys, grad_values, bias_terms = lax.map(one_sequence, (query_full, key_states, value_states, grad_output))
    grad_bias = lax.optimization_barrier(jnp.sum(bias_terms, axis=0))
    return (grad_queries, grad_keys, grad_values, grad_bias)
```

```python
import functools
import math

import jax
import jax.numpy as jnp
from jax import lax
from jax.experimental import pallas as pl
from jax.experimental.pallas import tpu as pltpu
from jax.sharding import PartitionSpec as P

HDIM = 128
TILE = 256
MASKED = -1e30


def _pack_kernel(*refs):
    out_ref = refs[-1]
    heads = out_ref.shape[0]
    for t, ref in enumerate(refs[:-1]):
        for h in range(heads):
            out_ref[h, t] = ref[0, :, h * HDIM : (h + 1) * HDIM]


def pack(arrays, item, step_heads):
    _, rows, width = arrays[0].shape
    heads = width // HDIM
    count = len(arrays)
    return pl.pallas_call(
        _pack_kernel,
        grid=(heads // step_heads,),
        in_specs=[
            pl.BlockSpec((1, rows, step_heads * HDIM), lambda c: (item, 0, c))
        ] * count,
        out_specs=pl.BlockSpec((step_heads, count, rows, HDIM), lambda c: (c, 0, 0, 0)),
        out_shape=jax.ShapeDtypeStruct((heads, count, rows, HDIM), arrays[0].dtype),
        cost_estimate=pl.CostEstimate(
            flops=0, bytes_accessed=4 * count * rows * width, transcendentals=0
        ),
        name="pack",
    )(*arrays)


def _unpack_kernel(count, in_ref, *refs):
    outs = refs[-count:]
    heads = in_ref.shape[0]
    for t, ref in enumerate(outs):
        for h in range(heads):
            ref[0, :, h * HDIM : (h + 1) * HDIM] = in_ref[h, t]


def unpack(packed, item, items, step_heads, into=None):
    heads, count, rows, _ = packed.shape
    width = heads * HDIM
    kwargs = {}
    operands = [packed]
    in_specs = [pl.BlockSpec((step_heads, count, rows, HDIM), lambda c: (c, 0, 0, 0))]
    if into is not None:
        operands += list(into)
        in_specs += [pl.BlockSpec(memory_space=pl.ANY)] * count
        kwargs["input_output_aliases"] = {1 + t: t for t in range(count)}
    return pl.pallas_call(
        functools.partial(_unpack_kernel, count),
        grid=(heads // step_heads,),
        in_specs=in_specs,
        out_specs=[
            pl.BlockSpec((1, rows, step_heads * HDIM), lambda c: (item, 0, c))
        ] * count,
        out_shape=[jax.ShapeDtypeStruct((items, rows, width), packed.dtype)] * count,
        cost_estimate=pl.CostEstimate(
            flops=0, bytes_accessed=4 * count * rows * width, transcendentals=0
        ),
        name="unpack",
        **kwargs,
    )(*operands)


def _dot_nt(a, b):
    return lax.dot_general(a, b, (((1,), (1,)), ((), ())), preferred_element_type=jnp.float32)


def _dot(a, b):
    return jnp.dot(a, b, preferred_element_type=jnp.float32)


def _fold(x, op):
    parts = [x[r : r + 8] for r in range(0, x.shape[0], 8)]
    while len(parts) > 1:
        parts = [op(a, b) for a, b in zip(parts[::2], parts[1::2])]
    return parts[0]


def _attend_kernel(x_ref, bias_ref, y_ref, sums_ref, q_s, kt_s, s_s, dp_s, dk_s, dv_s):
    peers, _, rows, _ = x_ref.shape
    blocks = peers * rows // TILE
    per = TILE // rows
    factor = 1.0 / math.sqrt(HDIM)

    def piece(t, i):
        return x_ref[i * per : (i + 1) * per, t].reshape(TILE, HDIM)

    for i in range(blocks):
        q_s[i] = (piece(0, i).astype(jnp.float32) + bias_ref[...]).astype(jnp.bfloat16)
        kt_s[i] = piece(1, i).T

    key_id = lax.broadcasted_iota(jnp.int32, (TILE, TILE), 0)
    query_id = lax.broadcasted_iota(jnp.int32, (TILE, TILE), 1)
    sums = jnp.zeros((8, HDIM), jnp.float32)
    for i in range(blocks):
        q_i = q_s[i]
        g_i = piece(3, i)
        top = None
        for j in range(i + 1):
            s = _dot_nt(piece(1, j), q_i) * factor
            if j == i:
                s = jnp.where(key_id <= query_id, s, MASKED)
            s_s[j] = s
            part = _fold(s, jnp.maximum)
            top = part if top is None else jnp.maximum(top, part)
        top = jnp.max(top, axis=0, keepdims=True)
        total = jnp.zeros((8, TILE), jnp.float32)
        row_dot = jnp.zeros((8, TILE), jnp.float32)
        for j in range(i + 1):
            e = jnp.exp(s_s[j] - top)
            dp = _dot_nt(piece(2, j), g_i)
            s_s[j] = e
            dp_s[j] = dp
            total = total + _fold(e, jnp.add)
            row_dot = row_dot + _fold(e * dp, jnp.add)
        inv = 1.0 / jnp.sum(total, axis=0, keepdims=True)
        row_dot = jnp.sum(row_dot, axis=0, keepdims=True) * inv
        dqt = None
        for j in range(i + 1):
            p = s_s[j] * inv
            ds = (p * (dp_s[j] - row_dot) * factor).astype(jnp.bfloat16)
            dv = _dot(p.astype(jnp.bfloat16), g_i)
            dk = _dot(ds, q_i)
            term = _dot(kt_s[j], ds)
            dqt = term if dqt is None else dqt + term
            if j == i:
                dv_s[j] = dv
                dk_s[j] = dk
            else:
                dv_s[j] += dv
                dk_s[j] += dk
        dq = dqt.T
        sums = sums + _fold(dq, jnp.add)
        y_ref[i * per : (i + 1) * per, 0] = dq.astype(jnp.bfloat16).reshape(per, rows, HDIM)
    for j in range(blocks):
        y_ref[j * per : (j + 1) * per, 1] = dk_s[j].astype(jnp.bfloat16).reshape(per, rows, HDIM)
        y_ref[j * per : (j + 1) * per, 2] = dv_s[j].astype(jnp.bfloat16).reshape(per, rows, HDIM)
    sums_ref[...] = jnp.sum(sums, axis=0, keepdims=True)


def attend(x, bias):
    peers, _, rows, _ = x.shape
    seq = peers * rows
    blocks = seq // TILE
    area = seq * (seq + TILE) // 2
    return pl.pallas_call(
        _attend_kernel,
        in_specs=[pl.BlockSpec(memory_space=pltpu.VMEM)] * 2,
        out_specs=[pl.BlockSpec(memory_space=pltpu.VMEM)] * 2,
        out_shape=[
            jax.ShapeDtypeStruct((peers, 3, rows, HDIM), jnp.bfloat16),
            jax.ShapeDtypeStruct((1, HDIM), jnp.float32),
        ],
        scratch_shapes=[
            pltpu.VMEM((blocks, TILE, HDIM), jnp.bfloat16),
            pltpu.VMEM((blocks, HDIM, TILE), jnp.bfloat16),
            pltpu.VMEM((blocks, TILE, TILE), jnp.float32),
            pltpu.VMEM((blocks, TILE, TILE), jnp.float32),
            pltpu.VMEM((blocks, TILE, HDIM), jnp.float32),
            pltpu.VMEM((blocks, TILE, HDIM), jnp.float32),
        ],
        compiler_params=pltpu.CompilerParams(vmem_limit_bytes=32 * 1024 * 1024),
        cost_estimate=pl.CostEstimate(
            flops=10 * area * HDIM * 2, bytes_accessed=14 * seq * HDIM, transcendentals=area
        ),
        name="attend",
    )(x, bias)


def spread_sum(x, size):
    step = 1
    while step < size:
        x = x + lax.ppermute(x, "dp", [(d, d ^ step) for d in range(size)])
        step *= 2
    return x


def body(queries, key_states, value_states, grad_output, query_bias, *, dp_size):
    items, rows, width = queries.shape
    inputs = (queries, key_states, value_states, grad_output)
    me = lax.axis_index("dp")
    share = query_bias.shape[0]

    own = lax.broadcasted_iota(jnp.int32, (dp_size, share), 0) == me
    slots = jnp.where(own, query_bias[None, :], jnp.zeros((), query_bias.dtype))
    bias = spread_sum(slots, dp_size).astype(jnp.float32).reshape(1, dp_size * share)

    sums = None
    results = []
    for item in range(items):
        packed = pack(inputs, item, 8)
        moved = lax.all_to_all(packed, "seq", split_axis=0, concat_axis=0, tiled=True)
        grads, part = attend(moved, bias)
        sums = part if sums is None else sums + part
        results.append(lax.all_to_all(grads, "seq", split_axis=0, concat_axis=0, tiled=True))
    outs = None
    for item, packed in enumerate(results):
        outs = unpack(packed, item, items, 8, into=outs)
    total = spread_sum(sums.reshape(dp_size, share), dp_size)
    grad_bias = lax.dynamic_index_in_dim(total, me, 0, keepdims=False)
    return (*outs, grad_bias)


def solution(mesh):
    rows = P("dp", "seq", None)
    cols = P(("seq", "dp"))
    return jax.shard_map(
        functools.partial(body, dp_size=mesh.shape["dp"]),
        mesh=mesh,
        in_specs=(rows, rows, rows, rows, cols),
        out_specs=(rows, rows, rows, cols),
        check_vma=False,
    )
```

```python
import functools
import math

import jax
import jax.numpy as jnp
from jax import lax
from jax.experimental import pallas as pl
from jax.experimental.pallas import tpu as pltpu
from jax.sharding import PartitionSpec as P

HDIM = 128
TILE = 256
MASKED = -1e30


def _pack_kernel(item, count, groups, *refs):
    srcs, out_ref = refs[:count], refs[count]
    in_s, out_s, in_sem, out_sem = refs[-4:]
    heads = out_ref.shape[0] // groups

    def load(c, t):
        cols = pl.ds(c * heads * HDIM, heads * HDIM)
        return pltpu.make_async_copy(
            srcs[t].at[item, :, cols], in_s.at[t, :, cols], in_sem.at[c, t]
        )

    def store(c):
        span = pl.ds(c * heads, heads)
        return pltpu.make_async_copy(out_s.at[span], out_ref.at[span], out_sem.at[c])

    for c in range(groups):
        for t in range(count):
            load(c, t).start()
    for c in range(groups):
        for t in range(count):
            load(c, t).wait()
            for h in range(c * heads, (c + 1) * heads):
                out_s[h, t] = in_s[t, :, h * HDIM : (h + 1) * HDIM]
        store(c).start()
    for c in range(groups):
        store(c).wait()


def pack(arrays, item, groups):
    _, rows, width = arrays[0].shape
    heads = width // HDIM
    count = len(arrays)
    dtype = arrays[0].dtype
    return pl.pallas_call(
        functools.partial(_pack_kernel, item, count, groups),
        in_specs=[pl.BlockSpec(memory_space=pl.ANY)] * count,
        out_specs=pl.BlockSpec(memory_space=pl.ANY),
        out_shape=jax.ShapeDtypeStruct((heads, count, rows, HDIM), dtype),
        scratch_shapes=[
            pltpu.VMEM((count, rows, width), dtype),
            pltpu.VMEM((heads, count, rows, HDIM), dtype),
            pltpu.SemaphoreType.DMA((groups, count)),
            pltpu.SemaphoreType.DMA((groups,)),
        ],
        cost_estimate=pl.CostEstimate(
            flops=0, bytes_accessed=4 * count * rows * width, transcendentals=0
        ),
        compiler_params=pltpu.CompilerParams(vmem_limit_bytes=56 * 1024 * 1024),
        name="pack",
    )(*arrays)


def _unpack_kernel(item, count, groups, *refs):
    in_ref, outs = refs[0], refs[-count - 2 : -2]
    out_s, out_sem = refs[-2:]
    heads = in_ref.shape[0] // groups

    def store(c, t):
        cols = pl.ds(c * heads * HDIM, heads * HDIM)
        return pltpu.make_async_copy(
            out_s.at[t, :, cols], outs[t].at[item, :, cols], out_sem.at[c, t]
        )

    for c in range(groups):
        for t in range(count):
            for h in range(c * heads, (c + 1) * heads):
                out_s[t, :, h * HDIM : (h + 1) * HDIM] = in_ref[h, t]
            store(c, t).start()
    for c in range(groups):
        for t in range(count):
            store(c, t).wait()


def unpack(packed, item, items, groups, into=None):
    heads, count, rows, _ = packed.shape
    width = heads * HDIM
    kwargs = {}
    operands = [packed]
    if into is not None:
        operands += list(into)
        kwargs["input_output_aliases"] = {1 + t: t for t in range(count)}
    return pl.pallas_call(
        functools.partial(_unpack_kernel, item, count, groups),
        in_specs=[pl.BlockSpec(memory_space=pltpu.VMEM)]
        + [pl.BlockSpec(memory_space=pl.ANY)] * (len(operands) - 1),
        out_specs=[pl.BlockSpec(memory_space=pl.ANY)] * count,
        out_shape=[jax.ShapeDtypeStruct((items, rows, width), packed.dtype)] * count,
        scratch_shapes=[
            pltpu.VMEM((count, rows, width), packed.dtype),
            pltpu.SemaphoreType.DMA((groups, count)),
        ],
        cost_estimate=pl.CostEstimate(
            flops=0, bytes_accessed=4 * count * rows * width, transcendentals=0
        ),
        compiler_params=pltpu.CompilerParams(vmem_limit_bytes=8 * 1024 * 1024),
        name="unpack",
        **kwargs,
    )(*operands)


def _dot_nt(a, b):
    return lax.dot_general(a, b, (((1,), (1,)), ((), ())), preferred_element_type=jnp.float32)


def _dot(a, b):
    return jnp.dot(a, b, preferred_element_type=jnp.float32)


def _fold(x, op):
    parts = [x[r : r + 8] for r in range(0, x.shape[0], 8)]
    while len(parts) > 1:
        parts = [op(a, b) for a, b in zip(parts[::2], parts[1::2])]
    return parts[0]


def _attend_kernel(x_ref, bias_ref, prior_ref, y_ref, sums_ref, q_s, kt_s, s_s, dp_s, dk_s, dv_s):
    peers, _, rows, _ = x_ref.shape
    blocks = peers * rows // TILE
    per = TILE // rows
    factor = 1.0 / math.sqrt(HDIM)

    def piece(t, i):
        return x_ref[i * per : (i + 1) * per, t].reshape(TILE, HDIM)

    for i in range(blocks):
        q_s[i] = (piece(0, i).astype(jnp.float32) + bias_ref[...]).astype(jnp.bfloat16)
        kt_s[i] = piece(1, i).T

    key_id = lax.broadcasted_iota(jnp.int32, (TILE, TILE), 0)
    query_id = lax.broadcasted_iota(jnp.int32, (TILE, TILE), 1)
    sums = prior_ref[...]
    for i in range(blocks):
        q_i = q_s[i]
        g_i = piece(3, i)
        top = None
        for j in range(i + 1):
            s = _dot_nt(piece(1, j), q_i) * factor
            if j == i:
                s = jnp.where(key_id <= query_id, s, MASKED)
            s_s[j] = s
            part = _fold(s, jnp.maximum)
            top = part if top is None else jnp.maximum(top, part)
        top = jnp.max(top, axis=0, keepdims=True)
        total = jnp.zeros((8, TILE), jnp.float32)
        row_dot = jnp.zeros((8, TILE), jnp.float32)
        for j in range(i + 1):
            e = jnp.exp(s_s[j] - top)
            dp = _dot_nt(piece(2, j), g_i)
            s_s[j] = e
            dp_s[j] = dp
            total = total + _fold(e, jnp.add)
            row_dot = row_dot + _fold(e * dp, jnp.add)
        inv = 1.0 / jnp.sum(total, axis=0, keepdims=True)
        row_dot = jnp.sum(row_dot, axis=0, keepdims=True) * inv
        dqt = None
        for j in range(i + 1):
            p = s_s[j] * inv
            ds = (p * (dp_s[j] - row_dot) * factor).astype(jnp.bfloat16)
            dv = _dot(p.astype(jnp.bfloat16), g_i)
            dk = _dot(ds, q_i)
            term = _dot(kt_s[j], ds)
            dqt = term if dqt is None else dqt + term
            if j == i:
                dv_s[j] = dv
                dk_s[j] = dk
            else:
                dv_s[j] += dv
                dk_s[j] += dk
        dq = dqt.T
        sums = sums + _fold(dq, jnp.add)
        y_ref[i * per : (i + 1) * per, 0] = dq.astype(jnp.bfloat16).reshape(per, rows, HDIM)
    for j in range(blocks):
        y_ref[j * per : (j + 1) * per, 1] = dk_s[j].astype(jnp.bfloat16).reshape(per, rows, HDIM)
        y_ref[j * per : (j + 1) * per, 2] = dv_s[j].astype(jnp.bfloat16).reshape(per, rows, HDIM)
    sums_ref[...] = sums


def attend(x, bias, prior):
    peers, _, rows, _ = x.shape
    seq = peers * rows
    blocks = seq // TILE
    area = seq * (seq + TILE) // 2
    return pl.pallas_call(
        _attend_kernel,
        in_specs=[pl.BlockSpec(memory_space=pltpu.VMEM)] * 3,
        out_specs=[pl.BlockSpec(memory_space=pltpu.VMEM)] * 2,
        out_shape=[
            jax.ShapeDtypeStruct((peers, 3, rows, HDIM), jnp.bfloat16),
            jax.ShapeDtypeStruct((8, HDIM), jnp.float32),
        ],
        scratch_shapes=[
            pltpu.VMEM((blocks, TILE, HDIM), jnp.bfloat16),
            pltpu.VMEM((blocks, HDIM, TILE), jnp.bfloat16),
            pltpu.VMEM((blocks, TILE, TILE), jnp.float32),
            pltpu.VMEM((blocks, TILE, TILE), jnp.float32),
            pltpu.VMEM((blocks, TILE, HDIM), jnp.float32),
            pltpu.VMEM((blocks, TILE, HDIM), jnp.float32),
        ],
        compiler_params=pltpu.CompilerParams(vmem_limit_bytes=32 * 1024 * 1024),
        cost_estimate=pl.CostEstimate(
            flops=10 * area * HDIM * 2, bytes_accessed=14 * seq * HDIM, transcendentals=area
        ),
        name="attend",
    )(x, bias, prior)


def spread_sum(x, size):
    pair = x + lax.ppermute(x, "dp", [(d, d ^ 1) for d in range(size)])
    parts = [pair]
    for step in range(2, size, 2):
        parts.append(lax.ppermute(pair, "dp", [(d, d ^ step) for d in range(size)]))
    return sum(parts[1:], parts[0])


def body(queries, key_states, value_states, grad_output, query_bias, *, dp_size):
    items, rows, width = queries.shape
    inputs = (queries, key_states, value_states, grad_output)
    share = query_bias.shape[0]
    me = lax.axis_index("dp")

    own = lax.broadcasted_iota(jnp.int32, (dp_size, share), 0) == me
    slots = jnp.where(own, query_bias[None, :], jnp.zeros((), query_bias.dtype))
    bias = spread_sum(slots, dp_size).astype(jnp.float32).reshape(1, dp_size * share)

    sums = jnp.zeros((8, HDIM), jnp.float32)
    results = []
    for item in range(items):
        packed = pack(inputs, item, 4)
        if item == 1:
            packed, bias = lax.optimization_barrier((packed, bias))
        moved = lax.all_to_all(packed, "seq", split_axis=0, concat_axis=0, tiled=True)
        grads, sums = attend(moved, bias, sums)
        results.append(lax.all_to_all(grads, "seq", split_axis=0, concat_axis=0, tiled=True))
    outs = None
    for item, packed in enumerate(results):
        outs = unpack(packed, item, items, 4, into=outs)
        if item == 0:
            outs, sums = lax.optimization_barrier((outs, sums))
    total = spread_sum(jnp.sum(sums, axis=0).reshape(dp_size, share), dp_size)
    grad_bias = lax.dynamic_index_in_dim(total, me, 0, keepdims=False)
    return (*outs, grad_bias)


def solution(mesh):
    rows = P("dp", "seq", None)
    cols = P(("seq", "dp"))
    return jax.shard_map(
        functools.partial(body, dp_size=mesh.shape["dp"]),
        mesh=mesh,
        in_specs=(rows, rows, rows, rows, cols),
        out_specs=(rows, rows, rows, cols),
        check_vma=False,
    )
```

```python
import functools
import math

import jax
import jax.numpy as jnp
from jax import lax
from jax.experimental import pallas as pl
from jax.experimental.pallas import tpu as pltpu
from jax.sharding import PartitionSpec as P

HDIM = 128
TILE = 256
MASKED = -1e30
IN_CHUNKS = ((0, 1),)
OUT_CHUNKS = ((0, 1),)
GATE = -1


def _pack_kernel(items, count, groups, *refs):
    srcs, out_ref = refs[:count], refs[count]
    in_s, out_s, in_sem, out_sem = refs[count + 1 :]
    heads = out_ref.shape[0] // groups

    def load(c, n, t):
        cols = pl.ds(c * heads * HDIM, heads * HDIM)
        return pltpu.make_async_copy(
            srcs[t].at[items[n], :, cols], in_s.at[n * count + t, :, cols], in_sem.at[c, n, t]
        )

    def store(c):
        span = pl.ds(c * heads, heads)
        return pltpu.make_async_copy(out_s.at[span], out_ref.at[span], out_sem.at[c])

    places = [(n, t) for n in range(len(items)) for t in range(count)]
    for c in range(groups):
        for n, t in places:
            load(c, n, t).start()
    for c in range(groups):
        for n, t in places:
            load(c, n, t).wait()
            for h in range(c * heads, (c + 1) * heads):
                out_s[h, n * count + t] = in_s[n * count + t, :, h * HDIM : (h + 1) * HDIM]
        store(c).start()
    for c in range(groups):
        store(c).wait()


def pack(arrays, items, groups):
    _, rows, width = arrays[0].shape
    heads = width // HDIM
    count = len(arrays)
    total = count * len(items)
    dtype = arrays[0].dtype
    return pl.pallas_call(
        functools.partial(_pack_kernel, items, count, groups),
        in_specs=[pl.BlockSpec(memory_space=pl.ANY)] * count,
        out_specs=pl.BlockSpec(memory_space=pl.ANY),
        out_shape=jax.ShapeDtypeStruct((heads, total, rows, HDIM), dtype),
        scratch_shapes=[
            pltpu.VMEM((total, rows, width), dtype),
            pltpu.VMEM((heads, total, rows, HDIM), dtype),
            pltpu.SemaphoreType.DMA((groups, len(items), count)),
            pltpu.SemaphoreType.DMA((groups,)),
        ],
        cost_estimate=pl.CostEstimate(
            flops=0, bytes_accessed=4 * total * rows * width, transcendentals=0
        ),
        compiler_params=pltpu.CompilerParams(vmem_limit_bytes=56 * 1024 * 1024),
        name="pack",
    )(*arrays)


def _unpack_kernel(items, count, groups, *refs):
    in_ref, outs = refs[0], refs[-count - 2 : -2]
    out_s, out_sem = refs[-2:]
    heads = in_ref.shape[0] // groups

    def store(c, n, t):
        cols = pl.ds(c * heads * HDIM, heads * HDIM)
        return pltpu.make_async_copy(
            out_s.at[n * count + t, :, cols], outs[t].at[items[n], :, cols], out_sem.at[c, n, t]
        )

    places = [(n, t) for n in range(len(items)) for t in range(count)]
    for c in range(groups):
        for n, t in places:
            for h in range(c * heads, (c + 1) * heads):
                out_s[n * count + t, :, h * HDIM : (h + 1) * HDIM] = in_ref[h, n * count + t]
            store(c, n, t).start()
    for c in range(groups):
        for n, t in places:
            store(c, n, t).wait()


def unpack(packed, items, count, all_items, groups, into=None):
    heads, total, rows, _ = packed.shape
    width = heads * HDIM
    kwargs = {}
    operands = [packed]
    if into is not None:
        operands += list(into)
        kwargs["input_output_aliases"] = {1 + t: t for t in range(count)}
    return pl.pallas_call(
        functools.partial(_unpack_kernel, items, count, groups),
        in_specs=[pl.BlockSpec(memory_space=pltpu.VMEM)]
        + [pl.BlockSpec(memory_space=pl.ANY)] * (len(operands) - 1),
        out_specs=[pl.BlockSpec(memory_space=pl.ANY)] * count,
        out_shape=[jax.ShapeDtypeStruct((all_items, rows, width), packed.dtype)] * count,
        scratch_shapes=[
            pltpu.VMEM((total, rows, width), packed.dtype),
            pltpu.SemaphoreType.DMA((groups, len(items), count)),
        ],
        cost_estimate=pl.CostEstimate(
            flops=0, bytes_accessed=4 * total * rows * width, transcendentals=0
        ),
        compiler_params=pltpu.CompilerParams(vmem_limit_bytes=8 * 1024 * 1024),
        name="unpack",
        **kwargs,
    )(*operands)


def _dot_nt(a, b):
    return lax.dot_general(a, b, (((1,), (1,)), ((), ())), preferred_element_type=jnp.float32)


def _dot(a, b):
    return jnp.dot(a, b, preferred_element_type=jnp.float32)


def _fold(x, op):
    parts = [x[r : r + 8] for r in range(0, x.shape[0], 8)]
    out = parts[0]
    for part in parts[1:]:
        out = op(out, part)
    return out


def _attend_kernel(
    items,
    x_hbm,
    bias_ref,
    prior_ref,
    y_hbm,
    sums_ref,
    x_ref,
    y_ref,
    q_s,
    kt_s,
    qt_s,
    gt_s,
    s_s,
    dp_s,
    dk_s,
    dv_s,
    in_sem,
    out_sem,
):
    peers, _, rows, _ = x_ref.shape
    blocks = peers * rows // TILE
    per = TILE // rows
    factor = 1.0 / math.sqrt(HDIM)
    scale = factor * math.log2(math.e)
    key_id = lax.broadcasted_iota(jnp.int32, (TILE, TILE), 0)
    query_id = lax.broadcasted_iota(jnp.int32, (TILE, TILE), 1)
    state = {}
    total_sums = [prior_ref[...]]

    def load(n, i):
        place = (pl.ds(i * per, per), pl.ds(4 * n, 4))
        return pltpu.make_async_copy(x_hbm.at[place], x_ref.at[place], in_sem.at[n, i])

    def store(n, i):
        place = (pl.ds(i * per, per), pl.ds(3 * n, 3))
        return pltpu.make_async_copy(y_ref.at[place], y_hbm.at[place], out_sem.at[n, i])

    def piece(n, t, i):
        return x_ref[i * per : (i + 1) * per, 4 * n + t].reshape(TILE, HDIM)

    def score(step, n, i, j):
        if j == 0:
            load(n, i).wait()
            q_s[n, i] = (piece(n, 0, i).astype(jnp.float32) + bias_ref[...]).astype(jnp.bfloat16)
            kt_s[n, i] = piece(n, 1, i).T
            qt_s[step % 3] = q_s[n, i].T
            gt_s[step % 3] = piece(n, 3, i).T
        s = _dot(piece(n, 1, j), qt_s[step % 3])
        if j == i:
            s = jnp.where(key_id <= query_id, s, MASKED)
        s_s[step % 3, j] = s
        part = _fold(s, jnp.maximum)
        top = part if j == 0 else jnp.maximum(state[step, "top"], part)
        if j == i:
            top = jnp.max(top, axis=0, keepdims=True) * scale
        state[step, "top"] = top

    def weigh(step, n, i, j):
        e = jnp.exp2(s_s[step % 3, j] * scale - state[step, "top"])
        dp = _dot(piece(n, 2, j), gt_s[step % 3])
        s_s[step % 3, j] = e
        dp_s[step % 2, j] = dp
        total, row_dot = _fold(e, jnp.add), _fold(e * dp, jnp.add)
        if j > 0:
            total, row_dot = total + state[step, "total"], row_dot + state[step, "dot"]
        if j == i:
            total = 1.0 / jnp.sum(total, axis=0, keepdims=True)
            row_dot = jnp.sum(row_dot, axis=0, keepdims=True) * total
        state[step, "total"], state[step, "dot"] = total, row_dot

    def spread(step, n, i, j):
        p = s_s[step % 3, j] * state[step, "total"]
        ds = (p * (dp_s[step % 2, j] - state[step, "dot"]) * factor).astype(jnp.bfloat16)
        dv = _dot_nt(gt_s[step % 3], p.astype(jnp.bfloat16))
        dk = _dot_nt(qt_s[step % 3], ds)
        dq = _dot(kt_s[n, j], ds)
        if j > 0:
            dq = state[step, "dq"] + dq
        state[step, "dq"] = dq
        if i < blocks - 1:
            if j == i:
                dv_s[n, j] = dv
                dk_s[n, j] = dk
            else:
                dv_s[n, j] += dv
                dk_s[n, j] += dk
        else:
            if j < i:
                dv = dv_s[n, j] + dv
                dk = dk_s[n, j] + dk
            span = slice(j * per, (j + 1) * per)
            y_ref[span, 3 * n + 1] = dk.T.astype(jnp.bfloat16).reshape(per, rows, HDIM)
            y_ref[span, 3 * n + 2] = dv.T.astype(jnp.bfloat16).reshape(per, rows, HDIM)
        if j == i:
            dq = dq.T
            total_sums[0] = total_sums[0] + _fold(dq, jnp.add)
            span = slice(i * per, (i + 1) * per)
            y_ref[span, 3 * n] = dq.astype(jnp.bfloat16).reshape(per, rows, HDIM)
        if i == blocks - 1:
            store(n, j).start()

    order = [(n, i) for n in range(items) for i in range(blocks)]
    for n, i in order:
        load(n, i).start()
    for step in range(len(order) + 2):
        stages = []
        for lag, fn in ((2, spread), (1, weigh), (0, score)):
            if 0 <= step - lag < len(order):
                stages.append((fn, step - lag, *order[step - lag]))
        for j in range(blocks):
            for fn, at, n, i in stages:
                if j <= i:
                    fn(at, n, i, j)
    sums_ref[...] = total_sums[0]
    for n, i in order:
        store(n, i).wait()


def attend(x, bias, prior, items):
    peers, _, rows, _ = x.shape
    seq = peers * rows
    blocks = seq // TILE
    area = items * seq * (seq + TILE) // 2
    return pl.pallas_call(
        functools.partial(_attend_kernel, items),
        in_specs=[pl.BlockSpec(memory_space=pl.ANY)] + [pl.BlockSpec(memory_space=pltpu.VMEM)] * 2,
        out_specs=[pl.BlockSpec(memory_space=pl.ANY), pl.BlockSpec(memory_space=pltpu.VMEM)],
        out_shape=[
            jax.ShapeDtypeStruct((peers, 3 * items, rows, HDIM), jnp.bfloat16),
            jax.ShapeDtypeStruct((8, HDIM), jnp.float32),
        ],
        scratch_shapes=[
            pltpu.VMEM(x.shape, x.dtype),
            pltpu.VMEM((peers, 3 * items, rows, HDIM), jnp.bfloat16),
            pltpu.VMEM((items, blocks, TILE, HDIM), jnp.bfloat16),
            pltpu.VMEM((items, blocks, HDIM, TILE), jnp.bfloat16),
            pltpu.VMEM((3, HDIM, TILE), jnp.bfloat16),
            pltpu.VMEM((3, HDIM, TILE), jnp.bfloat16),
            pltpu.VMEM((3, blocks, TILE, TILE), jnp.float32),
            pltpu.VMEM((2, blocks, TILE, TILE), jnp.float32),
            pltpu.VMEM((items, blocks, HDIM, TILE), jnp.float32),
            pltpu.VMEM((items, blocks, HDIM, TILE), jnp.float32),
            pltpu.SemaphoreType.DMA((items, blocks)),
            pltpu.SemaphoreType.DMA((items, blocks)),
        ],
        compiler_params=pltpu.CompilerParams(vmem_limit_bytes=56 * 1024 * 1024),
        cost_estimate=pl.CostEstimate(
            flops=10 * area * HDIM, bytes_accessed=14 * items * seq * HDIM, transcendentals=area
        ),
        name="attend",
    )(x, bias, prior)


def spread_sum(x, size):
    pair = x + lax.ppermute(x, "dp", [(d, d ^ 1) for d in range(size)])
    parts = [pair]
    for step in range(2, size, 2):
        parts.append(lax.ppermute(pair, "dp", [(d, d ^ step) for d in range(size)]))
    return sum(parts[1:], parts[0])


def body(queries, key_states, value_states, grad_output, query_bias, *, dp_size):
    items, rows, width = queries.shape
    inputs = (queries, key_states, value_states, grad_output)
    share = query_bias.shape[0]
    me = lax.axis_index("dp")

    own = lax.broadcasted_iota(jnp.int32, (dp_size, share), 0) == me
    slots = jnp.where(own, query_bias[None, :], jnp.zeros((), query_bias.dtype))
    bias = spread_sum(slots, dp_size).astype(jnp.float32).reshape(1, dp_size * share)

    sums = jnp.zeros((8, HDIM), jnp.float32)
    received = {}
    for first, chunk in enumerate(IN_CHUNKS):
        packed = pack(inputs, chunk, 4)
        if GATE == first:
            packed, bias = lax.optimization_barrier((packed, bias))
        moved = lax.all_to_all(packed, "seq", split_axis=0, concat_axis=0, tiled=True)
        for n, item in enumerate(chunk):
            received[item] = moved[:, 4 * n : 4 * n + 4]
    outs = None
    for chunk in OUT_CHUNKS:
        x = jnp.concatenate([received[item] for item in chunk], axis=1)
        grads, sums = attend(x, bias, sums, len(chunk))
        packed = lax.all_to_all(grads, "seq", split_axis=0, concat_axis=0, tiled=True)
        outs = unpack(packed, chunk, 3, items, 4, into=outs)
        if chunk[0] == 0 and len(OUT_CHUNKS) > 1:
            outs, sums = lax.optimization_barrier((outs, sums))
    total = spread_sum(jnp.sum(sums, axis=0).reshape(dp_size, share), dp_size)
    grad_bias = lax.dynamic_index_in_dim(total, me, 0, keepdims=False)
    return (*outs, grad_bias)


def solution(mesh):
    rows = P("dp", "seq", None)
    cols = P(("seq", "dp"))
    return jax.shard_map(
        functools.partial(body, dp_size=mesh.shape["dp"]),
        mesh=mesh,
        in_specs=(rows, rows, rows, rows, cols),
        out_specs=(rows, rows, rows, cols),
        check_vma=False,
    )
```

```python
import functools
import math

import jax
import jax.numpy as jnp
from jax import lax
from jax.experimental import pallas as pl
from jax.experimental.pallas import tpu as pltpu
from jax.sharding import PartitionSpec as P

HDIM = 128
TILE = 256
MASKED = -1e30


def _pack_kernel(item, count, groups, *refs):
    srcs, out_ref = refs[:count], refs[count]
    in_s, out_s, in_sem, out_sem = refs[-4:]
    heads = out_ref.shape[0] // groups

    def load(c, t):
        cols = pl.ds(c * heads * HDIM, heads * HDIM)
        return pltpu.make_async_copy(
            srcs[t].at[item, :, cols], in_s.at[t, :, cols], in_sem.at[c, t]
        )

    def store(c):
        span = pl.ds(c * heads, heads)
        return pltpu.make_async_copy(out_s.at[span], out_ref.at[span], out_sem.at[c])

    for c in range(groups):
        for t in range(count):
            load(c, t).start()
    for c in range(groups):
        for t in range(count):
            load(c, t).wait()
            for h in range(c * heads, (c + 1) * heads):
                out_s[h, t] = in_s[t, :, h * HDIM : (h + 1) * HDIM]
        store(c).start()
    for c in range(groups):
        store(c).wait()


def pack(arrays, item, groups):
    _, rows, width = arrays[0].shape
    heads = width // HDIM
    count = len(arrays)
    dtype = arrays[0].dtype
    return pl.pallas_call(
        functools.partial(_pack_kernel, item, count, groups),
        in_specs=[pl.BlockSpec(memory_space=pl.ANY)] * count,
        out_specs=pl.BlockSpec(memory_space=pl.ANY),
        out_shape=jax.ShapeDtypeStruct((heads, count, rows, HDIM), dtype),
        scratch_shapes=[
            pltpu.VMEM((count, rows, width), dtype),
            pltpu.VMEM((heads, count, rows, HDIM), dtype),
            pltpu.SemaphoreType.DMA((groups, count)),
            pltpu.SemaphoreType.DMA((groups,)),
        ],
        cost_estimate=pl.CostEstimate(
            flops=0, bytes_accessed=4 * count * rows * width, transcendentals=0
        ),
        compiler_params=pltpu.CompilerParams(vmem_limit_bytes=56 * 1024 * 1024),
        name="pack",
    )(*arrays)


def _unpack_kernel(item, count, groups, *refs):
    in_ref, outs = refs[0], refs[-count - 2 : -2]
    out_s, out_sem = refs[-2:]
    heads = in_ref.shape[0] // groups

    def store(c, t):
        cols = pl.ds(c * heads * HDIM, heads * HDIM)
        return pltpu.make_async_copy(
            out_s.at[t, :, cols], outs[t].at[item, :, cols], out_sem.at[c, t]
        )

    for c in range(groups):
        for t in range(count):
            for h in range(c * heads, (c + 1) * heads):
                out_s[t, :, h * HDIM : (h + 1) * HDIM] = in_ref[h, t]
            store(c, t).start()
    for c in range(groups):
        for t in range(count):
            store(c, t).wait()


def unpack(packed, item, items, groups, into=None):
    heads, count, rows, _ = packed.shape
    width = heads * HDIM
    kwargs = {}
    operands = [packed]
    if into is not None:
        operands += list(into)
        kwargs["input_output_aliases"] = {1 + t: t for t in range(count)}
    return pl.pallas_call(
        functools.partial(_unpack_kernel, item, count, groups),
        in_specs=[pl.BlockSpec(memory_space=pltpu.VMEM)]
        + [pl.BlockSpec(memory_space=pl.ANY)] * (len(operands) - 1),
        out_specs=[pl.BlockSpec(memory_space=pl.ANY)] * count,
        out_shape=[jax.ShapeDtypeStruct((items, rows, width), packed.dtype)] * count,
        scratch_shapes=[
            pltpu.VMEM((count, rows, width), packed.dtype),
            pltpu.SemaphoreType.DMA((groups, count)),
        ],
        cost_estimate=pl.CostEstimate(
            flops=0, bytes_accessed=4 * count * rows * width, transcendentals=0
        ),
        compiler_params=pltpu.CompilerParams(vmem_limit_bytes=8 * 1024 * 1024),
        name="unpack",
        **kwargs,
    )(*operands)


def _dot_nt(a, b):
    return lax.dot_general(a, b, (((1,), (1,)), ((), ())), preferred_element_type=jnp.float32)


def _dot(a, b):
    return jnp.dot(a, b, preferred_element_type=jnp.float32)


def _fold(x, op):
    parts = [x[r : r + 8] for r in range(0, x.shape[0], 8)]
    while len(parts) > 1:
        parts = [op(a, b) for a, b in zip(parts[::2], parts[1::2])]
    return parts[0]


def _attend_kernel(x_ref, bias_ref, prior_ref, y_ref, sums_ref, q_s, kt_s, s_s, dp_s, dk_s, dv_s):
    peers, _, rows, _ = x_ref.shape
    blocks = peers * rows // TILE
    per = TILE // rows
    factor = 1.0 / math.sqrt(HDIM)

    def piece(t, i):
        return x_ref[i * per : (i + 1) * per, t].reshape(TILE, HDIM)

    for i in range(blocks):
        q_s[i] = (piece(0, i).astype(jnp.float32) + bias_ref[...]).astype(jnp.bfloat16)
        kt_s[i] = piece(1, i).T

    key_id = lax.broadcasted_iota(jnp.int32, (TILE, TILE), 0)
    query_id = lax.broadcasted_iota(jnp.int32, (TILE, TILE), 1)
    sums = prior_ref[...]
    for i in range(blocks):
        q_i = q_s[i]
        g_i = piece(3, i)
        top = None
        for j in range(i + 1):
            s = _dot_nt(piece(1, j), q_i) * factor
            if j == i:
                s = jnp.where(key_id <= query_id, s, MASKED)
            s_s[j] = s
            part = _fold(s, jnp.maximum)
            top = part if top is None else jnp.maximum(top, part)
        top = jnp.max(top, axis=0, keepdims=True)
        total = jnp.zeros((8, TILE), jnp.float32)
        row_dot = jnp.zeros((8, TILE), jnp.float32)
        for j in range(i + 1):
            e = jnp.exp(s_s[j] - top)
            dp = _dot_nt(piece(2, j), g_i)
            s_s[j] = e
            dp_s[j] = dp
            total = total + _fold(e, jnp.add)
            row_dot = row_dot + _fold(e * dp, jnp.add)
        inv = 1.0 / jnp.sum(total, axis=0, keepdims=True)
        row_dot = jnp.sum(row_dot, axis=0, keepdims=True) * inv
        dqt = None
        for j in range(i + 1):
            p = s_s[j] * inv
            ds = (p * (dp_s[j] - row_dot) * factor).astype(jnp.bfloat16)
            dv = _dot(p.astype(jnp.bfloat16), g_i)
            dk = _dot(ds, q_i)
            term = _dot(kt_s[j], ds)
            dqt = term if dqt is None else dqt + term
            if j == i:
                dv_s[j] = dv
                dk_s[j] = dk
            else:
                dv_s[j] += dv
                dk_s[j] += dk
        dq = dqt.T
        sums = sums + _fold(dq, jnp.add)
        y_ref[i * per : (i + 1) * per, 0] = dq.astype(jnp.bfloat16).reshape(per, rows, HDIM)
    for j in range(blocks):
        y_ref[j * per : (j + 1) * per, 1] = dk_s[j].astype(jnp.bfloat16).reshape(per, rows, HDIM)
        y_ref[j * per : (j + 1) * per, 2] = dv_s[j].astype(jnp.bfloat16).reshape(per, rows, HDIM)
    sums_ref[...] = sums


def attend(x, bias, prior):
    peers, _, rows, _ = x.shape
    seq = peers * rows
    blocks = seq // TILE
    area = seq * (seq + TILE) // 2
    return pl.pallas_call(
        _attend_kernel,
        in_specs=[pl.BlockSpec(memory_space=pltpu.VMEM)] * 3,
        out_specs=[pl.BlockSpec(memory_space=pltpu.VMEM)] * 2,
        out_shape=[
            jax.ShapeDtypeStruct((peers, 3, rows, HDIM), jnp.bfloat16),
            jax.ShapeDtypeStruct((8, HDIM), jnp.float32),
        ],
        scratch_shapes=[
            pltpu.VMEM((blocks, TILE, HDIM), jnp.bfloat16),
            pltpu.VMEM((blocks, HDIM, TILE), jnp.bfloat16),
            pltpu.VMEM((blocks, TILE, TILE), jnp.float32),
            pltpu.VMEM((blocks, TILE, TILE), jnp.float32),
            pltpu.VMEM((blocks, TILE, HDIM), jnp.float32),
            pltpu.VMEM((blocks, TILE, HDIM), jnp.float32),
        ],
        compiler_params=pltpu.CompilerParams(vmem_limit_bytes=62 * 1024 * 1024),
        cost_estimate=pl.CostEstimate(
            flops=10 * area * HDIM * 2, bytes_accessed=14 * seq * HDIM, transcendentals=area
        ),
        name="attend",
    )(x, bias, prior)


def spread_sum(x, size):
    pair = x + lax.ppermute(x, "dp", [(d, d ^ 1) for d in range(size)])
    parts = [pair]
    for step in range(2, size, 2):
        parts.append(lax.ppermute(pair, "dp", [(d, d ^ step) for d in range(size)]))
    return sum(parts[1:], parts[0])


def body(queries, key_states, value_states, grad_output, query_bias, *, dp_size):
    items, rows, width = queries.shape
    inputs = (queries, key_states, value_states, grad_output)
    share = query_bias.shape[0]
    me = lax.axis_index("dp")

    own = lax.broadcasted_iota(jnp.int32, (dp_size, share), 0) == me
    slots = jnp.where(own, query_bias[None, :], jnp.zeros((), query_bias.dtype))
    bias = spread_sum(slots, dp_size).astype(jnp.float32).reshape(1, dp_size * share)

    sums = jnp.zeros((8, HDIM), jnp.float32)
    results = []
    for item in range(items):
        packed = pack(inputs, item, 4)
        if item == 0:
            packed, bias = lax.optimization_barrier((packed, bias))
        moved = lax.all_to_all(packed, "seq", split_axis=0, concat_axis=0, tiled=True)
        grads, sums = attend(moved, bias, sums)
        results.append(lax.all_to_all(grads, "seq", split_axis=0, concat_axis=0, tiled=True))
    outs = None
    for item, packed in enumerate(results):
        outs = unpack(packed, item, items, 4, into=outs)
        if item == 0:
            outs, sums = lax.optimization_barrier((outs, sums))
    total = spread_sum(jnp.sum(sums, axis=0).reshape(dp_size, share), dp_size)
    grad_bias = lax.dynamic_index_in_dim(total, me, 0, keepdims=False)
    return (*outs, grad_bias)


def solution(mesh):
    rows = P("dp", "seq", None)
    cols = P(("seq", "dp"))
    return jax.shard_map(
        functools.partial(body, dp_size=mesh.shape["dp"]),
        mesh=mesh,
        in_specs=(rows, rows, rows, rows, cols),
        out_specs=(rows, rows, rows, cols),
        check_vma=False,
    )
```

```python
import functools
import math

import jax
import jax.numpy as jnp
from jax import lax
from jax.experimental import pallas as pl
from jax.experimental.pallas import tpu as pltpu
from jax.sharding import PartitionSpec as P

HDIM = 128
TILE = 256
MASKED = -1e30


def _pack_kernel(item, count, groups, *refs):
    srcs, out_ref = refs[:count], refs[count]
    in_s, out_s, in_sem, out_sem = refs[-4:]
    heads = out_ref.shape[0] // groups

    def load(c, t):
        cols = pl.ds(c * heads * HDIM, heads * HDIM)
        return pltpu.make_async_copy(
            srcs[t].at[item, :, cols], in_s.at[t, :, cols], in_sem.at[c, t]
        )

    def store(c):
        span = pl.ds(c * heads, heads)
        return pltpu.make_async_copy(out_s.at[span], out_ref.at[span], out_sem.at[c])

    for c in range(groups):
        for t in range(count):
            load(c, t).start()
    for c in range(groups):
        for t in range(count):
            load(c, t).wait()
            for h in range(c * heads, (c + 1) * heads):
                out_s[h, t] = in_s[t, :, h * HDIM : (h + 1) * HDIM]
        store(c).start()
    for c in range(groups):
        store(c).wait()


def pack(arrays, item, groups):
    _, rows, width = arrays[0].shape
    heads = width // HDIM
    count = len(arrays)
    dtype = arrays[0].dtype
    return pl.pallas_call(
        functools.partial(_pack_kernel, item, count, groups),
        in_specs=[pl.BlockSpec(memory_space=pl.ANY)] * count,
        out_specs=pl.BlockSpec(memory_space=pl.ANY),
        out_shape=jax.ShapeDtypeStruct((heads, count, rows, HDIM), dtype),
        scratch_shapes=[
            pltpu.VMEM((count, rows, width), dtype),
            pltpu.VMEM((heads, count, rows, HDIM), dtype),
            pltpu.SemaphoreType.DMA((groups, count)),
            pltpu.SemaphoreType.DMA((groups,)),
        ],
        cost_estimate=pl.CostEstimate(
            flops=0, bytes_accessed=4 * count * rows * width, transcendentals=0
        ),
        compiler_params=pltpu.CompilerParams(vmem_limit_bytes=56 * 1024 * 1024),
        name="pack",
    )(*arrays)


def _unpack_kernel(item, count, groups, *refs):
    in_ref, outs = refs[0], refs[-count - 2 : -2]
    out_s, out_sem = refs[-2:]
    heads = in_ref.shape[0] // groups

    def store(c, t):
        cols = pl.ds(c * heads * HDIM, heads * HDIM)
        return pltpu.make_async_copy(
            out_s.at[t, :, cols], outs[t].at[item, :, cols], out_sem.at[c, t]
        )

    for c in range(groups):
        for t in range(count):
            for h in range(c * heads, (c + 1) * heads):
                out_s[t, :, h * HDIM : (h + 1) * HDIM] = in_ref[h, t]
            store(c, t).start()
    for c in range(groups):
        for t in range(count):
            store(c, t).wait()


def unpack(packed, item, items, groups, into=None):
    heads, count, rows, _ = packed.shape
    width = heads * HDIM
    kwargs = {}
    operands = [packed]
    if into is not None:
        operands += list(into)
        kwargs["input_output_aliases"] = {1 + t: t for t in range(count)}
    return pl.pallas_call(
        functools.partial(_unpack_kernel, item, count, groups),
        in_specs=[pl.BlockSpec(memory_space=pltpu.VMEM)]
        + [pl.BlockSpec(memory_space=pl.ANY)] * (len(operands) - 1),
        out_specs=[pl.BlockSpec(memory_space=pl.ANY)] * count,
        out_shape=[jax.ShapeDtypeStruct((items, rows, width), packed.dtype)] * count,
        scratch_shapes=[
            pltpu.VMEM((count, rows, width), packed.dtype),
            pltpu.SemaphoreType.DMA((groups, count)),
        ],
        cost_estimate=pl.CostEstimate(
            flops=0, bytes_accessed=4 * count * rows * width, transcendentals=0
        ),
        compiler_params=pltpu.CompilerParams(vmem_limit_bytes=8 * 1024 * 1024),
        name="unpack",
        **kwargs,
    )(*operands)


def _dot_nt(a, b):
    return lax.dot_general(a, b, (((1,), (1,)), ((), ())), preferred_element_type=jnp.float32)


def _dot(a, b):
    return jnp.dot(a, b, preferred_element_type=jnp.float32)


def _fold(x, op):
    parts = [x[r : r + 8] for r in range(0, x.shape[0], 8)]
    while len(parts) > 1:
        parts = [op(a, b) for a, b in zip(parts[::2], parts[1::2])]
    return parts[0]


def _attend_kernel(x_ref, bias_ref, prior_ref, y_ref, sums_ref, q_s, kt_s, s_s, dp_s, dk_s, dv_s):
    peers, _, rows, _ = x_ref.shape
    blocks = peers * rows // TILE
    per = TILE // rows
    factor = 1.0 / math.sqrt(HDIM)

    def piece(t, i):
        return x_ref[i * per : (i + 1) * per, t].reshape(TILE, HDIM)

    for i in range(blocks):
        q_s[i] = (piece(0, i).astype(jnp.float32) + bias_ref[...]).astype(jnp.bfloat16)
        kt_s[i] = piece(1, i).T

    key_id = lax.broadcasted_iota(jnp.int32, (TILE, TILE), 0)
    query_id = lax.broadcasted_iota(jnp.int32, (TILE, TILE), 1)
    sums = prior_ref[...]
    for i in range(blocks):
        q_i = q_s[i]
        g_i = piece(3, i)
        top = None
        for j in range(i + 1):
            s = _dot_nt(piece(1, j), q_i) * factor
            if j == i:
                s = jnp.where(key_id <= query_id, s, MASKED)
            s_s[j] = s
            part = _fold(s, jnp.maximum)
            top = part if top is None else jnp.maximum(top, part)
        top = jnp.max(top, axis=0, keepdims=True)
        total = jnp.zeros((8, TILE), jnp.float32)
        row_dot = jnp.zeros((8, TILE), jnp.float32)
        for j in range(i + 1):
            e = jnp.exp(s_s[j] - top)
            dp = _dot_nt(piece(2, j), g_i)
            s_s[j] = e
            dp_s[j] = dp
            total = total + _fold(e, jnp.add)
            row_dot = row_dot + _fold(e * dp, jnp.add)
        inv = 1.0 / jnp.sum(total, axis=0, keepdims=True)
        row_dot = jnp.sum(row_dot, axis=0, keepdims=True) * inv
        dqt = None
        for j in range(i + 1):
            p = s_s[j] * inv
            ds = (p * (dp_s[j] - row_dot) * factor).astype(jnp.bfloat16)
            dv = _dot(p.astype(jnp.bfloat16), g_i)
            dk = _dot(ds, q_i)
            term = _dot(kt_s[j], ds)
            dqt = term if dqt is None else dqt + term
            if j == i:
                dv_s[j] = dv
                dk_s[j] = dk
            else:
                dv_s[j] += dv
                dk_s[j] += dk
        dq = dqt.T
        sums = sums + _fold(dq, jnp.add)
        y_ref[i * per : (i + 1) * per, 0] = dq.astype(jnp.bfloat16).reshape(per, rows, HDIM)
    for j in range(blocks):
        y_ref[j * per : (j + 1) * per, 1] = dk_s[j].astype(jnp.bfloat16).reshape(per, rows, HDIM)
        y_ref[j * per : (j + 1) * per, 2] = dv_s[j].astype(jnp.bfloat16).reshape(per, rows, HDIM)
    sums_ref[...] = sums


def attend(x, bias, prior):
    peers, _, rows, _ = x.shape
    seq = peers * rows
    blocks = seq // TILE
    area = seq * (seq + TILE) // 2
    return pl.pallas_call(
        _attend_kernel,
        in_specs=[pl.BlockSpec(memory_space=pltpu.VMEM)] * 3,
        out_specs=[pl.BlockSpec(memory_space=pltpu.VMEM)] * 2,
        out_shape=[
            jax.ShapeDtypeStruct((peers, 3, rows, HDIM), jnp.bfloat16),
            jax.ShapeDtypeStruct((8, HDIM), jnp.float32),
        ],
        scratch_shapes=[
            pltpu.VMEM((blocks, TILE, HDIM), jnp.bfloat16),
            pltpu.VMEM((blocks, HDIM, TILE), jnp.bfloat16),
            pltpu.VMEM((blocks, TILE, TILE), jnp.float32),
            pltpu.VMEM((blocks, TILE, TILE), jnp.float32),
            pltpu.VMEM((blocks, TILE, HDIM), jnp.float32),
            pltpu.VMEM((blocks, TILE, HDIM), jnp.float32),
        ],
        compiler_params=pltpu.CompilerParams(vmem_limit_bytes=32 * 1024 * 1024),
        cost_estimate=pl.CostEstimate(
            flops=10 * area * HDIM * 2, bytes_accessed=14 * seq * HDIM, transcendentals=area
        ),
        name="attend",
    )(x, bias, prior)


def spread_sum(x, size):
    pair = x + lax.ppermute(x, "dp", [(d, d ^ 1) for d in range(size)])
    parts = [pair]
    for step in range(2, size, 2):
        parts.append(lax.ppermute(pair, "dp", [(d, d ^ step) for d in range(size)]))
    return sum(parts[1:], parts[0])


def body(queries, key_states, value_states, grad_output, query_bias, *, dp_size):
    items, rows, width = queries.shape
    inputs = (queries, key_states, value_states, grad_output)
    share = query_bias.shape[0]
    me = lax.axis_index("dp")

    lanes = dp_size * share
    wide = jnp.tile(query_bias.astype(jnp.float32), dp_size).reshape(1, lanes)
    own = lax.broadcasted_iota(jnp.int32, (HDIM, lanes), 1) // share == me
    slots = jnp.where(own, jnp.broadcast_to(wide, (HDIM, lanes)), 0.0)
    bias = lax.psum(slots, "dp")[:1]

    sums = jnp.zeros((8, HDIM), jnp.float32)
    results = []
    for item in range(items):
        packed = pack(inputs, item, 4)
        if item == 1:
            packed, bias = lax.optimization_barrier((packed, bias))
        moved = lax.all_to_all(packed, "seq", split_axis=0, concat_axis=0, tiled=True)
        grads, sums = attend(moved, bias, sums)
        results.append(lax.all_to_all(grads, "seq", split_axis=0, concat_axis=0, tiled=True))
    outs = None
    for item, packed in enumerate(results):
        outs = unpack(packed, item, items, 4, into=outs)
        if item == 0:
            outs, sums = lax.optimization_barrier((outs, sums))
    total = spread_sum(jnp.sum(sums, axis=0).reshape(dp_size, share), dp_size)
    grad_bias = lax.dynamic_index_in_dim(total, me, 0, keepdims=False)
    return (*outs, grad_bias)


def solution(mesh):
    rows = P("dp", "seq", None)
    cols = P(("seq", "dp"))
    return jax.shard_map(
        functools.partial(body, dp_size=mesh.shape["dp"]),
        mesh=mesh,
        in_specs=(rows, rows, rows, rows, cols),
        out_specs=(rows, rows, rows, cols),
        check_vma=False,
    )
```

```python
import functools
import math

import jax
import jax.numpy as jnp
from jax import lax
from jax.experimental import pallas as pl
from jax.experimental.pallas import tpu as pltpu
from jax.sharding import PartitionSpec as P

HDIM = 128
TILE = 256
MASKED = -1e30
OUT_CHUNKS = ((0,), (1,))


def _pack_kernel(items, count, groups, *refs):
    srcs, out_ref = refs[:count], refs[count]
    in_s, out_s, in_sem, out_sem = refs[count + 1 :]
    heads = out_ref.shape[0] // groups

    def load(c, n, t):
        cols = pl.ds(c * heads * HDIM, heads * HDIM)
        return pltpu.make_async_copy(
            srcs[t].at[items[n], :, cols], in_s.at[n * count + t, :, cols], in_sem.at[c, n, t]
        )

    def store(c):
        span = pl.ds(c * heads, heads)
        return pltpu.make_async_copy(out_s.at[span], out_ref.at[span], out_sem.at[c])

    places = [(n, t) for n in range(len(items)) for t in range(count)]
    for c in range(groups):
        for n, t in places:
            load(c, n, t).start()
    for c in range(groups):
        for n, t in places:
            load(c, n, t).wait()
            for h in range(c * heads, (c + 1) * heads):
                out_s[h, n * count + t] = in_s[n * count + t, :, h * HDIM : (h + 1) * HDIM]
        store(c).start()
    for c in range(groups):
        store(c).wait()


def pack(arrays, items, groups):
    _, rows, width = arrays[0].shape
    heads = width // HDIM
    count = len(arrays)
    total = count * len(items)
    dtype = arrays[0].dtype
    return pl.pallas_call(
        functools.partial(_pack_kernel, items, count, groups),
        in_specs=[pl.BlockSpec(memory_space=pl.ANY)] * count,
        out_specs=pl.BlockSpec(memory_space=pl.ANY),
        out_shape=jax.ShapeDtypeStruct((heads, total, rows, HDIM), dtype),
        scratch_shapes=[
            pltpu.VMEM((total, rows, width), dtype),
            pltpu.VMEM((heads, total, rows, HDIM), dtype),
            pltpu.SemaphoreType.DMA((groups, len(items), count)),
            pltpu.SemaphoreType.DMA((groups,)),
        ],
        cost_estimate=pl.CostEstimate(
            flops=0, bytes_accessed=4 * total * rows * width, transcendentals=0
        ),
        compiler_params=pltpu.CompilerParams(vmem_limit_bytes=56 * 1024 * 1024),
        name="pack",
    )(*arrays)


def _unpack_kernel(items, count, groups, *refs):
    in_ref, outs = refs[0], refs[-count - 2 : -2]
    out_s, out_sem = refs[-2:]
    heads = in_ref.shape[0] // groups

    def store(c, n, t):
        cols = pl.ds(c * heads * HDIM, heads * HDIM)
        return pltpu.make_async_copy(
            out_s.at[n * count + t, :, cols], outs[t].at[items[n], :, cols], out_sem.at[c, n, t]
        )

    places = [(n, t) for n in range(len(items)) for t in range(count)]
    for c in range(groups):
        for n, t in places:
            for h in range(c * heads, (c + 1) * heads):
                out_s[n * count + t, :, h * HDIM : (h + 1) * HDIM] = in_ref[h, n * count + t]
            store(c, n, t).start()
    for c in range(groups):
        for n, t in places:
            store(c, n, t).wait()


def unpack(packed, items, count, all_items, groups, into=None):
    heads, total, rows, _ = packed.shape
    width = heads * HDIM
    kwargs = {}
    operands = [packed]
    if into is not None:
        operands += list(into)
        kwargs["input_output_aliases"] = {1 + t: t for t in range(count)}
    return pl.pallas_call(
        functools.partial(_unpack_kernel, items, count, groups),
        in_specs=[pl.BlockSpec(memory_space=pltpu.VMEM)]
        + [pl.BlockSpec(memory_space=pl.ANY)] * (len(operands) - 1),
        out_specs=[pl.BlockSpec(memory_space=pl.ANY)] * count,
        out_shape=[jax.ShapeDtypeStruct((all_items, rows, width), packed.dtype)] * count,
        scratch_shapes=[
            pltpu.VMEM((total, rows, width), packed.dtype),
            pltpu.SemaphoreType.DMA((groups, len(items), count)),
        ],
        cost_estimate=pl.CostEstimate(
            flops=0, bytes_accessed=4 * total * rows * width, transcendentals=0
        ),
        compiler_params=pltpu.CompilerParams(vmem_limit_bytes=8 * 1024 * 1024),
        name="unpack",
        **kwargs,
    )(*operands)


def _dot_nt(a, b):
    return lax.dot_general(a, b, (((1,), (1,)), ((), ())), preferred_element_type=jnp.float32)


def _dot(a, b):
    return jnp.dot(a, b, preferred_element_type=jnp.float32)


def _fold(x, op):
    parts = [x[r : r + 8] for r in range(0, x.shape[0], 8)]
    out = parts[0]
    for part in parts[1:]:
        out = op(out, part)
    return out


def _attend_kernel(
    items,
    first,
    x_hbm,
    bias_ref,
    prior_ref,
    y_hbm,
    sums_ref,
    x_ref,
    y_ref,
    q_s,
    kt_s,
    qt_s,
    gt_s,
    s_s,
    dp_s,
    dk_s,
    dv_s,
    in_sem,
    out_sem,
):
    peers, _, rows, _ = x_ref.shape
    blocks = peers * rows // TILE
    per = TILE // rows
    factor = 1.0 / math.sqrt(HDIM)
    scale = factor * math.log2(math.e)
    key_id = lax.broadcasted_iota(jnp.int32, (TILE, TILE), 0)
    query_id = lax.broadcasted_iota(jnp.int32, (TILE, TILE), 1)
    state = {}
    total_sums = [prior_ref[...]]

    def load(n, i):
        span = pl.ds(i * per, per)
        return pltpu.make_async_copy(
            x_hbm.at[span, pl.ds(4 * (first + n), 4)],
            x_ref.at[span, pl.ds(4 * n, 4)],
            in_sem.at[n, i],
        )

    def store(n, i):
        place = (pl.ds(i * per, per), pl.ds(3 * n, 3))
        return pltpu.make_async_copy(y_ref.at[place], y_hbm.at[place], out_sem.at[n, i])

    def piece(n, t, i):
        return x_ref[i * per : (i + 1) * per, 4 * n + t].reshape(TILE, HDIM)

    def score(step, n, i, j):
        if j == 0:
            load(n, i).wait()
            q_s[n, i] = (piece(n, 0, i).astype(jnp.float32) + bias_ref[...]).astype(jnp.bfloat16)
            kt_s[n, i] = piece(n, 1, i).T
            qt_s[step % 3] = q_s[n, i].T
            gt_s[step % 3] = piece(n, 3, i).T
        s = _dot(piece(n, 1, j), qt_s[step % 3])
        if j == i:
            s = jnp.where(key_id <= query_id, s, MASKED)
        s_s[step % 3, j] = s
        part = _fold(s, jnp.maximum)
        top = part if j == 0 else jnp.maximum(state[step, "top"], part)
        if j == i:
            top = jnp.max(top, axis=0, keepdims=True) * scale
        state[step, "top"] = top

    def weigh(step, n, i, j):
        e = jnp.exp2(s_s[step % 3, j] * scale - state[step, "top"])
        dp = _dot(piece(n, 2, j), gt_s[step % 3])
        s_s[step % 3, j] = e
        dp_s[step % 2, j] = dp
        total, row_dot = _fold(e, jnp.add), _fold(e * dp, jnp.add)
        if j > 0:
            total, row_dot = total + state[step, "total"], row_dot + state[step, "dot"]
        if j == i:
            total = 1.0 / jnp.sum(total, axis=0, keepdims=True)
            row_dot = jnp.sum(row_dot, axis=0, keepdims=True) * total
        state[step, "total"], state[step, "dot"] = total, row_dot

    def spread(step, n, i, j):
        p = s_s[step % 3, j] * state[step, "total"]
        ds = (p * (dp_s[step % 2, j] - state[step, "dot"]) * factor).astype(jnp.bfloat16)
        dv = _dot_nt(gt_s[step % 3], p.astype(jnp.bfloat16))
        dk = _dot_nt(qt_s[step % 3], ds)
        dq = _dot(kt_s[n, j], ds)
        if j > 0:
            dq = state[step, "dq"] + dq
        state[step, "dq"] = dq
        if i < blocks - 1:
            if j == i:
                dv_s[n, j] = dv
                dk_s[n, j] = dk
            else:
                dv_s[n, j] += dv
                dk_s[n, j] += dk
        else:
            if j < i:
                dv = dv_s[n, j] + dv
                dk = dk_s[n, j] + dk
            span = slice(j * per, (j + 1) * per)
            y_ref[span, 3 * n + 1] = dk.T.astype(jnp.bfloat16).reshape(per, rows, HDIM)
            y_ref[span, 3 * n + 2] = dv.T.astype(jnp.bfloat16).reshape(per, rows, HDIM)
        if j == i:
            dq = dq.T
            total_sums[0] = total_sums[0] + _fold(dq, jnp.add)
            span = slice(i * per, (i + 1) * per)
            y_ref[span, 3 * n] = dq.astype(jnp.bfloat16).reshape(per, rows, HDIM)
        if i == blocks - 1:
            store(n, j).start()

    order = [(n, i) for n in range(items) for i in range(blocks)]
    for n, i in order:
        load(n, i).start()
    for step in range(len(order) + 2):
        stages = []
        for lag, fn in ((2, spread), (1, weigh), (0, score)):
            if 0 <= step - lag < len(order):
                stages.append((fn, step - lag, *order[step - lag]))
        for j in range(blocks):
            for fn, at, n, i in stages:
                if j <= i:
                    fn(at, n, i, j)
    sums_ref[...] = total_sums[0]
    for n, i in order:
        store(n, i).wait()


def attend(x, bias, prior, first, items):
    peers, _, rows, _ = x.shape
    seq = peers * rows
    blocks = seq // TILE
    area = items * seq * (seq + TILE) // 2
    return pl.pallas_call(
        functools.partial(_attend_kernel, items, first),
        in_specs=[pl.BlockSpec(memory_space=pl.ANY)] + [pl.BlockSpec(memory_space=pltpu.VMEM)] * 2,
        out_specs=[pl.BlockSpec(memory_space=pl.ANY), pl.BlockSpec(memory_space=pltpu.VMEM)],
        out_shape=[
            jax.ShapeDtypeStruct((peers, 3 * items, rows, HDIM), jnp.bfloat16),
            jax.ShapeDtypeStruct((8, HDIM), jnp.float32),
        ],
        scratch_shapes=[
            pltpu.VMEM((peers, 4 * items, rows, HDIM), x.dtype),
            pltpu.VMEM((peers, 3 * items, rows, HDIM), jnp.bfloat16),
            pltpu.VMEM((items, blocks, TILE, HDIM), jnp.bfloat16),
            pltpu.VMEM((items, blocks, HDIM, TILE), jnp.bfloat16),
            pltpu.VMEM((3, HDIM, TILE), jnp.bfloat16),
            pltpu.VMEM((3, HDIM, TILE), jnp.bfloat16),
            pltpu.VMEM((3, blocks, TILE, TILE), jnp.float32),
            pltpu.VMEM((2, blocks, TILE, TILE), jnp.float32),
            pltpu.VMEM((items, blocks, HDIM, TILE), jnp.float32),
            pltpu.VMEM((items, blocks, HDIM, TILE), jnp.float32),
            pltpu.SemaphoreType.DMA((items, blocks)),
            pltpu.SemaphoreType.DMA((items, blocks)),
        ],
        compiler_params=pltpu.CompilerParams(vmem_limit_bytes=56 * 1024 * 1024),
        cost_estimate=pl.CostEstimate(
            flops=10 * area * HDIM, bytes_accessed=14 * items * seq * HDIM, transcendentals=area
        ),
        name="attend",
    )(x, bias, prior)


def pair_sum(x, size):
    return x + lax.ppermute(x, "dp", [(d, d ^ 1) for d in range(size)])


def others(pair, size):
    return [
        lax.ppermute(pair, "dp", [(d, d ^ step) for d in range(size)])
        for step in range(2, size, 2)
    ]


def body(queries, key_states, value_states, grad_output, query_bias, *, dp_size):
    items, rows, width = queries.shape
    inputs = (queries, key_states, value_states, grad_output)
    share = query_bias.shape[0]
    me = lax.axis_index("dp")

    own = lax.broadcasted_iota(jnp.int32, (dp_size, share), 0) == me
    slots = jnp.where(own, query_bias[None, :], jnp.zeros((), query_bias.dtype))
    pair = pair_sum(slots, dp_size)
    parts = others(pair, dp_size)

    packed = pack(inputs, tuple(range(items)), 4)
    moved = lax.all_to_all(packed, "seq", split_axis=0, concat_axis=0, tiled=True)
    moved, pair = lax.optimization_barrier((moved, pair))
    bias = sum(parts, pair).astype(jnp.float32).reshape(1, dp_size * share)

    sums = jnp.zeros((8, HDIM), jnp.float32)
    results = []
    for chunk in OUT_CHUNKS:
        grads, sums = attend(moved, bias, sums, chunk[0], len(chunk))
        results.append(lax.all_to_all(grads, "seq", split_axis=0, concat_axis=0, tiled=True))
    outs = None
    for chunk, packed in zip(OUT_CHUNKS, results):
        outs = unpack(packed, chunk, 3, items, 4, into=outs)
        if chunk[-1] < items - 1:
            outs, sums = lax.optimization_barrier((outs, sums))
    pair = pair_sum(jnp.sum(sums, axis=0).reshape(dp_size, share), dp_size)
    total = sum(others(pair, dp_size), pair)
    grad_bias = lax.dynamic_index_in_dim(total, me, 0, keepdims=False)
    return (*outs, grad_bias)


def solution(mesh):
    rows = P("dp", "seq", None)
    cols = P(("seq", "dp"))
    return jax.shard_map(
        functools.partial(body, dp_size=mesh.shape["dp"]),
        mesh=mesh,
        in_specs=(rows, rows, rows, rows, cols),
        out_specs=(rows, rows, rows, cols),
        check_vma=False,
    )
```

```python
import functools
import math

import jax
import jax.numpy as jnp
from jax import lax
from jax.experimental import pallas as pl
from jax.experimental.pallas import tpu as pltpu
from jax.sharding import PartitionSpec as P

HDIM = 128
TILE = 256
MASKED = -1e30


def _pack_kernel(item, count, groups, *refs):
    srcs, out_ref = refs[:count], refs[count]
    in_s, out_s, in_sem, out_sem = refs[-4:]
    heads = out_ref.shape[0] // groups

    def load(c, t):
        cols = pl.ds(c * heads * HDIM, heads * HDIM)
        return pltpu.make_async_copy(
            srcs[t].at[item, :, cols], in_s.at[t, :, cols], in_sem.at[c, t]
        )

    def store(c):
        span = pl.ds(c * heads, heads)
        return pltpu.make_async_copy(out_s.at[span], out_ref.at[span], out_sem.at[c])

    for c in range(groups):
        for t in range(count):
            load(c, t).start()
    for c in range(groups):
        for t in range(count):
            load(c, t).wait()
            for h in range(c * heads, (c + 1) * heads):
                out_s[h, t] = in_s[t, :, h * HDIM : (h + 1) * HDIM]
        store(c).start()
    for c in range(groups):
        store(c).wait()


def pack(arrays, item, groups):
    _, rows, width = arrays[0].shape
    heads = width // HDIM
    count = len(arrays)
    dtype = arrays[0].dtype
    return pl.pallas_call(
        functools.partial(_pack_kernel, item, count, groups),
        in_specs=[pl.BlockSpec(memory_space=pl.ANY)] * count,
        out_specs=pl.BlockSpec(memory_space=pl.ANY),
        out_shape=jax.ShapeDtypeStruct((heads, count, rows, HDIM), dtype),
        scratch_shapes=[
            pltpu.VMEM((count, rows, width), dtype),
            pltpu.VMEM((heads, count, rows, HDIM), dtype),
            pltpu.SemaphoreType.DMA((groups, count)),
            pltpu.SemaphoreType.DMA((groups,)),
        ],
        cost_estimate=pl.CostEstimate(
            flops=0, bytes_accessed=4 * count * rows * width, transcendentals=0
        ),
        compiler_params=pltpu.CompilerParams(vmem_limit_bytes=56 * 1024 * 1024),
        name="pack",
    )(*arrays)


def _unpack_kernel(item, count, groups, *refs):
    in_ref, outs = refs[0], refs[-count - 2 : -2]
    out_s, out_sem = refs[-2:]
    heads = in_ref.shape[0] // groups

    def store(c, t):
        cols = pl.ds(c * heads * HDIM, heads * HDIM)
        return pltpu.make_async_copy(
            out_s.at[t, :, cols], outs[t].at[item, :, cols], out_sem.at[c, t]
        )

    for c in range(groups):
        for t in range(count):
            for h in range(c * heads, (c + 1) * heads):
                out_s[t, :, h * HDIM : (h + 1) * HDIM] = in_ref[h, t]
            store(c, t).start()
    for c in range(groups):
        for t in range(count):
            store(c, t).wait()


def unpack(packed, item, items, groups, into=None):
    heads, count, rows, _ = packed.shape
    width = heads * HDIM
    kwargs = {}
    operands = [packed]
    if into is not None:
        operands += list(into)
        kwargs["input_output_aliases"] = {1 + t: t for t in range(count)}
    return pl.pallas_call(
        functools.partial(_unpack_kernel, item, count, groups),
        in_specs=[pl.BlockSpec(memory_space=pltpu.VMEM)]
        + [pl.BlockSpec(memory_space=pl.ANY)] * (len(operands) - 1),
        out_specs=[pl.BlockSpec(memory_space=pl.ANY)] * count,
        out_shape=[jax.ShapeDtypeStruct((items, rows, width), packed.dtype)] * count,
        scratch_shapes=[
            pltpu.VMEM((count, rows, width), packed.dtype),
            pltpu.SemaphoreType.DMA((groups, count)),
        ],
        cost_estimate=pl.CostEstimate(
            flops=0, bytes_accessed=4 * count * rows * width, transcendentals=0
        ),
        compiler_params=pltpu.CompilerParams(vmem_limit_bytes=8 * 1024 * 1024),
        name="unpack",
        **kwargs,
    )(*operands)


def _dot_nt(a, b):
    return lax.dot_general(a, b, (((1,), (1,)), ((), ())), preferred_element_type=jnp.float32)


def _dot(a, b):
    return jnp.dot(a, b, preferred_element_type=jnp.float32)


def _fold(x, op):
    parts = [x[r : r + 8] for r in range(0, x.shape[0], 8)]
    while len(parts) > 1:
        parts = [op(a, b) for a, b in zip(parts[::2], parts[1::2])]
    return parts[0]


def _attend_kernel(x_ref, bias_ref, prior_ref, y_ref, sums_ref, q_s, kt_s, s_s, dp_s, dk_s, dv_s):
    peers, _, rows, _ = x_ref.shape
    blocks = peers * rows // TILE
    per = TILE // rows
    factor = 1.0 / math.sqrt(HDIM)

    def piece(t, i):
        return x_ref[i * per : (i + 1) * per, t].reshape(TILE, HDIM)

    for i in range(blocks):
        q_s[i] = (piece(0, i).astype(jnp.float32) + bias_ref[...]).astype(jnp.bfloat16)
        kt_s[i] = piece(1, i).T

    key_id = lax.broadcasted_iota(jnp.int32, (TILE, TILE), 0)
    query_id = lax.broadcasted_iota(jnp.int32, (TILE, TILE), 1)
    sums = prior_ref[...]
    for i in range(blocks):
        q_i = q_s[i]
        g_i = piece(3, i)
        top = None
        for j in range(i + 1):
            s = _dot_nt(piece(1, j), q_i) * factor
            if j == i:
                s = jnp.where(key_id <= query_id, s, MASKED)
            s_s[j] = s
            part = _fold(s, jnp.maximum)
            top = part if top is None else jnp.maximum(top, part)
        top = jnp.max(top, axis=0, keepdims=True)
        total = jnp.zeros((8, TILE), jnp.float32)
        row_dot = jnp.zeros((8, TILE), jnp.float32)
        for j in range(i + 1):
            e = jnp.exp(s_s[j] - top)
            dp = _dot_nt(piece(2, j), g_i)
            s_s[j] = e
            dp_s[j] = dp
            total = total + _fold(e, jnp.add)
            row_dot = row_dot + _fold(e * dp, jnp.add)
        inv = 1.0 / jnp.sum(total, axis=0, keepdims=True)
        row_dot = jnp.sum(row_dot, axis=0, keepdims=True) * inv
        dqt = None
        for j in range(i + 1):
            p = s_s[j] * inv
            ds = (p * (dp_s[j] - row_dot) * factor).astype(jnp.bfloat16)
            dv = _dot(p.astype(jnp.bfloat16), g_i)
            dk = _dot(ds, q_i)
            term = _dot(kt_s[j], ds)
            dqt = term if dqt is None else dqt + term
            if j == i:
                dv_s[j] = dv
                dk_s[j] = dk
            else:
                dv_s[j] += dv
                dk_s[j] += dk
        dq = dqt.T
        sums = sums + _fold(dq, jnp.add)
        y_ref[i * per : (i + 1) * per, 0] = dq.astype(jnp.bfloat16).reshape(per, rows, HDIM)
    for j in range(blocks):
        y_ref[j * per : (j + 1) * per, 1] = dk_s[j].astype(jnp.bfloat16).reshape(per, rows, HDIM)
        y_ref[j * per : (j + 1) * per, 2] = dv_s[j].astype(jnp.bfloat16).reshape(per, rows, HDIM)
    sums_ref[...] = sums


def attend(x, bias, prior):
    peers, _, rows, _ = x.shape
    seq = peers * rows
    blocks = seq // TILE
    area = seq * (seq + TILE) // 2
    return pl.pallas_call(
        _attend_kernel,
        in_specs=[pl.BlockSpec(memory_space=pltpu.VMEM)] * 3,
        out_specs=[pl.BlockSpec(memory_space=pltpu.VMEM)] * 2,
        out_shape=[
            jax.ShapeDtypeStruct((peers, 3, rows, HDIM), jnp.bfloat16),
            jax.ShapeDtypeStruct((8, HDIM), jnp.float32),
        ],
        scratch_shapes=[
            pltpu.VMEM((blocks, TILE, HDIM), jnp.bfloat16),
            pltpu.VMEM((blocks, HDIM, TILE), jnp.bfloat16),
            pltpu.VMEM((blocks, TILE, TILE), jnp.float32),
            pltpu.VMEM((blocks, TILE, TILE), jnp.float32),
            pltpu.VMEM((blocks, TILE, HDIM), jnp.float32),
            pltpu.VMEM((blocks, TILE, HDIM), jnp.float32),
        ],
        compiler_params=pltpu.CompilerParams(vmem_limit_bytes=32 * 1024 * 1024),
        cost_estimate=pl.CostEstimate(
            flops=10 * area * HDIM * 2, bytes_accessed=14 * seq * HDIM, transcendentals=area
        ),
        name="attend",
    )(x, bias, prior)


def pair_sum(x, size):
    return x + lax.ppermute(x, "dp", [(d, d ^ 1) for d in range(size)])


def spread_sum(pair, size):
    parts = [pair]
    for step in range(2, size, 2):
        parts.append(lax.ppermute(pair, "dp", [(d, d ^ step) for d in range(size)]))
    return sum(parts[1:], parts[0])


def body(queries, key_states, value_states, grad_output, query_bias, *, dp_size):
    items, rows, width = queries.shape
    inputs = (queries, key_states, value_states, grad_output)
    share = query_bias.shape[0]
    me = lax.axis_index("dp")

    own = lax.broadcasted_iota(jnp.int32, (dp_size, share), 0) == me
    slots = jnp.where(own, query_bias[None, :], jnp.zeros((), query_bias.dtype))
    first, pair = lax.optimization_barrier((pack(inputs, 0, 4), pair_sum(slots, dp_size)))
    bias = spread_sum(pair, dp_size).astype(jnp.float32).reshape(1, dp_size * share)

    sums = jnp.zeros((8, HDIM), jnp.float32)
    results = []
    for item in range(items):
        packed = first if item == 0 else pack(inputs, item, 4)
        if item == 1:
            packed, bias = lax.optimization_barrier((packed, bias))
        moved = lax.all_to_all(packed, "seq", split_axis=0, concat_axis=0, tiled=True)
        grads, sums = attend(moved, bias, sums)
        results.append(lax.all_to_all(grads, "seq", split_axis=0, concat_axis=0, tiled=True))
    outs = None
    for item, packed in enumerate(results):
        outs = unpack(packed, item, items, 4, into=outs)
        if item == 0:
            outs, sums = lax.optimization_barrier((outs, sums))
    total = spread_sum(pair_sum(jnp.sum(sums, axis=0).reshape(dp_size, share), dp_size), dp_size)
    grad_bias = lax.dynamic_index_in_dim(total, me, 0, keepdims=False)
    return (*outs, grad_bias)


def solution(mesh):
    rows = P("dp", "seq", None)
    cols = P(("seq", "dp"))
    return jax.shard_map(
        functools.partial(body, dp_size=mesh.shape["dp"]),
        mesh=mesh,
        in_specs=(rows, rows, rows, rows, cols),
        out_specs=(rows, rows, rows, cols),
        check_vma=False,
    )
```

```python
import functools
import math

import jax
import jax.numpy as jnp
from jax import lax
from jax.experimental import pallas as pl
from jax.experimental.pallas import tpu as pltpu
from jax.sharding import PartitionSpec as P

HDIM = 128
TILE = 256
MASKED = -1e30


def _pack_kernel(item, count, groups, *refs):
    srcs, out_ref = refs[:count], refs[count]
    in_s, out_s, in_sem, out_sem = refs[-4:]
    heads = out_ref.shape[0] // groups

    def load(c, t):
        cols = pl.ds(c * heads * HDIM, heads * HDIM)
        return pltpu.make_async_copy(
            srcs[t].at[item, :, cols], in_s.at[t, :, cols], in_sem.at[c, t]
        )

    def store(c):
        span = pl.ds(c * heads, heads)
        return pltpu.make_async_copy(out_s.at[span], out_ref.at[span], out_sem.at[c])

    for c in range(groups):
        for t in range(count):
            load(c, t).start()
    for c in range(groups):
        for t in range(count):
            load(c, t).wait()
            for h in range(c * heads, (c + 1) * heads):
                out_s[h, t] = in_s[t, :, h * HDIM : (h + 1) * HDIM]
        store(c).start()
    for c in range(groups):
        store(c).wait()


def pack(arrays, item, groups):
    _, rows, width = arrays[0].shape
    heads = width // HDIM
    count = len(arrays)
    dtype = arrays[0].dtype
    return pl.pallas_call(
        functools.partial(_pack_kernel, item, count, groups),
        in_specs=[pl.BlockSpec(memory_space=pl.ANY)] * count,
        out_specs=pl.BlockSpec(memory_space=pl.ANY),
        out_shape=jax.ShapeDtypeStruct((heads, count, rows, HDIM), dtype),
        scratch_shapes=[
            pltpu.VMEM((count, rows, width), dtype),
            pltpu.VMEM((heads, count, rows, HDIM), dtype),
            pltpu.SemaphoreType.DMA((groups, count)),
            pltpu.SemaphoreType.DMA((groups,)),
        ],
        cost_estimate=pl.CostEstimate(
            flops=0, bytes_accessed=4 * count * rows * width, transcendentals=0
        ),
        compiler_params=pltpu.CompilerParams(vmem_limit_bytes=56 * 1024 * 1024),
        name="pack",
    )(*arrays)


def _unpack_kernel(item, count, groups, *refs):
    in_ref, outs = refs[0], refs[-count - 2 : -2]
    out_s, out_sem = refs[-2:]
    heads = in_ref.shape[0] // groups

    def store(c, t):
        cols = pl.ds(c * heads * HDIM, heads * HDIM)
        return pltpu.make_async_copy(
            out_s.at[t, :, cols], outs[t].at[item, :, cols], out_sem.at[c, t]
        )

    for c in range(groups):
        for t in range(count):
            for h in range(c * heads, (c + 1) * heads):
                out_s[t, :, h * HDIM : (h + 1) * HDIM] = in_ref[h, t]
            store(c, t).start()
    for c in range(groups):
        for t in range(count):
            store(c, t).wait()


def unpack(packed, item, items, groups, into=None):
    heads, count, rows, _ = packed.shape
    width = heads * HDIM
    kwargs = {}
    operands = [packed]
    if into is not None:
        operands += list(into)
        kwargs["input_output_aliases"] = {1 + t: t for t in range(count)}
    return pl.pallas_call(
        functools.partial(_unpack_kernel, item, count, groups),
        in_specs=[pl.BlockSpec(memory_space=pltpu.VMEM)]
        + [pl.BlockSpec(memory_space=pl.ANY)] * (len(operands) - 1),
        out_specs=[pl.BlockSpec(memory_space=pl.ANY)] * count,
        out_shape=[jax.ShapeDtypeStruct((items, rows, width), packed.dtype)] * count,
        scratch_shapes=[
            pltpu.VMEM((count, rows, width), packed.dtype),
            pltpu.SemaphoreType.DMA((groups, count)),
        ],
        cost_estimate=pl.CostEstimate(
            flops=0, bytes_accessed=4 * count * rows * width, transcendentals=0
        ),
        compiler_params=pltpu.CompilerParams(vmem_limit_bytes=8 * 1024 * 1024),
        name="unpack",
        **kwargs,
    )(*operands)


def _dot_nt(a, b):
    return lax.dot_general(a, b, (((1,), (1,)), ((), ())), preferred_element_type=jnp.float32)


def _dot(a, b):
    return jnp.dot(a, b, preferred_element_type=jnp.float32)


def _fold(x, op):
    parts = [x[r : r + 8] for r in range(0, x.shape[0], 8)]
    while len(parts) > 1:
        parts = [op(a, b) for a, b in zip(parts[::2], parts[1::2])]
    return parts[0]


def _attend_kernel(x_ref, bias_ref, prior_ref, y_ref, sums_ref, q_s, kt_s, s_s, dp_s, dk_s, dv_s):
    peers, _, rows, _ = x_ref.shape
    blocks = peers * rows // TILE
    per = TILE // rows
    factor = 1.0 / math.sqrt(HDIM)

    def piece(t, i):
        return x_ref[i * per : (i + 1) * per, t].reshape(TILE, HDIM)

    for i in range(blocks):
        q_s[i] = (piece(0, i).astype(jnp.float32) + bias_ref[...]).astype(jnp.bfloat16)
        kt_s[i] = piece(1, i).T

    key_id = lax.broadcasted_iota(jnp.int32, (TILE, TILE), 0)
    query_id = lax.broadcasted_iota(jnp.int32, (TILE, TILE), 1)
    sums = prior_ref[...]
    for i in range(blocks):
        q_i = q_s[i]
        g_i = piece(3, i)
        top = None
        for j in range(i + 1):
            s = _dot_nt(piece(1, j), q_i) * factor
            if j == i:
                s = jnp.where(key_id <= query_id, s, MASKED)
            s_s[j] = s
            part = _fold(s, jnp.maximum)
            top = part if top is None else jnp.maximum(top, part)
        top = jnp.max(top, axis=0, keepdims=True)
        total = jnp.zeros((8, TILE), jnp.float32)
        row_dot = jnp.zeros((8, TILE), jnp.float32)
        for j in range(i + 1):
            e = jnp.exp(s_s[j] - top)
            dp = _dot_nt(piece(2, j), g_i)
            s_s[j] = e
            dp_s[j] = dp
            total = total + _fold(e, jnp.add)
            row_dot = row_dot + _fold(e * dp, jnp.add)
        inv = 1.0 / jnp.sum(total, axis=0, keepdims=True)
        row_dot = jnp.sum(row_dot, axis=0, keepdims=True) * inv
        dqt = None
        for j in range(i + 1):
            p = s_s[j] * inv
            ds = (p * (dp_s[j] - row_dot) * factor).astype(jnp.bfloat16)
            dv = _dot(p.astype(jnp.bfloat16), g_i)
            dk = _dot(ds, q_i)
            term = _dot(kt_s[j], ds)
            dqt = term if dqt is None else dqt + term
            if j == i:
                dv_s[j] = dv
                dk_s[j] = dk
            else:
                dv_s[j] += dv
                dk_s[j] += dk
        dq = dqt.T
        sums = sums + _fold(dq, jnp.add)
        y_ref[i * per : (i + 1) * per, 0] = dq.astype(jnp.bfloat16).reshape(per, rows, HDIM)
    for j in range(blocks):
        y_ref[j * per : (j + 1) * per, 1] = dk_s[j].astype(jnp.bfloat16).reshape(per, rows, HDIM)
        y_ref[j * per : (j + 1) * per, 2] = dv_s[j].astype(jnp.bfloat16).reshape(per, rows, HDIM)
    sums_ref[...] = sums


def attend(x, bias, prior):
    peers, _, rows, _ = x.shape
    seq = peers * rows
    blocks = seq // TILE
    area = seq * (seq + TILE) // 2
    return pl.pallas_call(
        _attend_kernel,
        in_specs=[pl.BlockSpec(memory_space=pltpu.VMEM)] * 3,
        out_specs=[pl.BlockSpec(memory_space=pltpu.VMEM)] * 2,
        out_shape=[
            jax.ShapeDtypeStruct((peers, 3, rows, HDIM), jnp.bfloat16),
            jax.ShapeDtypeStruct((8, HDIM), jnp.float32),
        ],
        scratch_shapes=[
            pltpu.VMEM((blocks, TILE, HDIM), jnp.bfloat16),
            pltpu.VMEM((blocks, HDIM, TILE), jnp.bfloat16),
            pltpu.VMEM((blocks, TILE, TILE), jnp.float32),
            pltpu.VMEM((blocks, TILE, TILE), jnp.float32),
            pltpu.VMEM((blocks, TILE, HDIM), jnp.float32),
            pltpu.VMEM((blocks, TILE, HDIM), jnp.float32),
        ],
        compiler_params=pltpu.CompilerParams(vmem_limit_bytes=32 * 1024 * 1024),
        cost_estimate=pl.CostEstimate(
            flops=10 * area * HDIM * 2, bytes_accessed=14 * seq * HDIM, transcendentals=area
        ),
        name="attend",
    )(x, bias, prior)


def spread_sum(x, size):
    pair = x + lax.ppermute(x, "dp", [(d, d ^ 1) for d in range(size)])
    parts = [pair]
    for step in range(2, size, 2):
        parts.append(lax.ppermute(pair, "dp", [(d, d ^ step) for d in range(size)]))
    return sum(parts[1:], parts[0])


def shared_sum(x, size, ahead):
    swap = [(d, d ^ 1) for d in range(size)]
    pair = x + lax.ppermute(x, "dp", swap)
    pair, ahead = lax.optimization_barrier((pair, ahead))
    got = None
    for even, odd in ((2, 4), (6, None)):
        moves = [(d, d ^ even) for d in range(0, size, 2)]
        if odd is not None:
            moves += [(d, d ^ odd) for d in range(1, size, 2)]
        part = lax.ppermute(pair, "dp", moves)
        got = part if got is None else got + part
    return pair + got + lax.ppermute(got, "dp", swap), ahead


def body(queries, key_states, value_states, grad_output, query_bias, *, dp_size):
    items, rows, width = queries.shape
    inputs = (queries, key_states, value_states, grad_output)
    share = query_bias.shape[0]
    me = lax.axis_index("dp")

    own = lax.broadcasted_iota(jnp.int32, (dp_size, share), 0) == me
    slots = jnp.where(own, query_bias[None, :], jnp.zeros((), query_bias.dtype))
    bias, second = shared_sum(slots, dp_size, pack(inputs, 1, 4))
    bias = bias.astype(jnp.float32).reshape(1, dp_size * share)

    sums = jnp.zeros((8, HDIM), jnp.float32)
    results = []
    for item in range(items):
        packed = second if item == 1 else pack(inputs, item, 4)
        if item == 1:
            packed, bias = lax.optimization_barrier((packed, bias))
        moved = lax.all_to_all(packed, "seq", split_axis=0, concat_axis=0, tiled=True)
        grads, sums = attend(moved, bias, sums)
        results.append(lax.all_to_all(grads, "seq", split_axis=0, concat_axis=0, tiled=True))
    outs = None
    for item, packed in enumerate(results):
        outs = unpack(packed, item, items, 4, into=outs)
        if item == 0:
            outs, sums = lax.optimization_barrier((outs, sums))
    total = spread_sum(jnp.sum(sums, axis=0).reshape(dp_size, share), dp_size)
    grad_bias = lax.dynamic_index_in_dim(total, me, 0, keepdims=False)
    return (*outs, grad_bias)


def solution(mesh):
    rows = P("dp", "seq", None)
    cols = P(("seq", "dp"))
    return jax.shard_map(
        functools.partial(body, dp_size=mesh.shape["dp"]),
        mesh=mesh,
        in_specs=(rows, rows, rows, rows, cols),
        out_specs=(rows, rows, rows, cols),
        check_vma=False,
    )
```
